256 devices in a mesh: group: 16 (over y, x), member: 16 (over z, core).
Axes of the slice: x: 4, y: 4, z: 8, core: 2. Of those that a mesh axis runs over, the one named last changes fastest.
Arguments:
- test_points: bfloat16 [256, 3, 1024], P(('group', 'member')), may hold values from 0 to 4
- test_basis: bfloat16 [256, 2, 1024, 256], P(('group', 'member')), may hold values from -0.25 to 0.25
- source_points: bfloat16 [256, 3, 1024], P(('group', 'member')), may hold values from 0 to 4
- source_basis: bfloat16 [256, 2, 1024, 256], P(('group', 'member')), may hold values from -0.1875 to 0.1875
- excitation: bfloat16 [256, 2, 256, 256], P(('group', 'member')), may hold values from -6 to 6
- preconditioner: bfloat16 [256, 256, 2, 256], P(('group', 'member')), may hold values from -0.25 to 0.25
- plan: int32 [2, 2], replicated, may hold values from 0 to 255, as said below
- solver_owner: int32 [256, 2, 4], P(('group', 'member')), may hold values from 0 to 15, as said below
Outputs:
- result: float32 [256, 256, 2, 256], P(('group', 'member'))
The draws below stay inside these ranges and needn't reach their ends.
Inputs may be any that keep to these rules, and one draw needn't show every extreme that they name: `plan`: distinct domain indices. `solver_owner`: owners lie in the tile's own group. At most 2 of one device's 8 tiles go to one owner; in every group one owner takes exactly 2 tiles from every device of the group.
All inputs are finite; a program needn't handle non-finite values.
Results may differ from the reference program's by a relative error of at most 0.008.
Values may be sent and summed in bfloat16 or wider, within the bound.
A program may use at most 128 MiB of HBM per device.

```python
import math
import jax
import jax.numpy as jnp
from jax import lax

NB = 256
EXC = 256
SRC_PTS = 1024
TEST_DEV = 1024
DOM_DEV = 2
DOM_PTS = 512
ROUNDS = 2
PER_ROUND = 2
DOMAINS = 256
N_MEMBER = 16


def draw_plan(key, part):
    inner = jax.random.permutation(jax.random.fold_in(key, 11), DOMAINS - 2) + 1
    ends = jnp.array([0, DOMAINS - 1], dtype=jnp.int32)
    picked = jnp.concatenate([ends, inner[:ROUNDS * PER_ROUND - 2].astype(jnp.int32)])
    order = jax.random.permutation(jax.random.fold_in(key, 12), ROUNDS * PER_ROUND)
    return picked[order].reshape(ROUNDS, PER_ROUND).astype(jnp.int32)


def draw_solver_owner(key, part):
    tile_count = DOM_DEV * ROUNDS * PER_ROUND
    groups = DOMAINS // N_MEMBER
    hottest = jax.random.randint(jax.random.fold_in(key, 21), (groups,), 0, N_MEMBER)
    hot_each = jnp.repeat(hottest, N_MEMBER)

    def one_domain(subkey, hot_member):
        key_one, key_two, key_three = jax.random.split(subkey, 3)
        others = (hot_member + 1 + jax.random.permutation(key_one, N_MEMBER - 1)) % N_MEMBER
        paired = jax.random.randint(key_two, (), 0, 2)
        head = jnp.stack([hot_member, hot_member])
        spread = jnp.concatenate([head, others[:tile_count - 2]])
        doubled = jnp.concatenate([head, jnp.repeat(others[:(tile_count - 2) // 2], 2)])
        picked = jnp.where(paired == 1, doubled, spread)
        order = jax.random.permutation(key_three, tile_count)
        return picked[order]
    keys = jax.random.split(jax.random.fold_in(key, 22), DOMAINS)
    flat = jax.vmap(one_domain)(keys, hot_each)
    return flat.reshape(DOMAINS, DOM_DEV, ROUNDS * PER_ROUND).astype(jnp.int32)


def level_of(rng, dims, cuts, least, high):
    def one(dim, parts):
        draws = jax.random.uniform(jax.random.fold_in(jax.random.fold_in(rng, 6), dim), (parts,), jnp.float32, least / len(cuts), high / len(cuts))
        return jnp.repeat(jnp.exp(draws), dims[dim] // parts).reshape((-1,) + (1,) * (len(dims) - dim - 1))

    loudness = one(*cuts[0])
    for cut in cuts[1:]:
        loudness = loudness * one(*cut)
    return loudness


def normal_values(stream_key, extent, scale, bound, cuts=(), kind=jnp.bfloat16):
    level = level_of(stream_key, extent, cuts, -0.22, 0.18) if cuts else 1.0
    result = jax.random.normal(stream_key, extent, jnp.float32) * scale * level
    return jnp.minimum(jnp.maximum(result, -bound), bound).astype(kind)


def setup_inputs(seed: int = 0) -> dict:
    splits = jax.random.split(jax.random.key(seed), 9)
    test_points = jnp.clip(4.0 * jax.random.uniform(splits[0], (DOMAINS, 3, TEST_DEV), jnp.float32) ** level_of(splits[0], (DOMAINS, 3, TEST_DEV), ((0, 256),), -0.2, 0.2), 0.0, 4.0).astype(jnp.bfloat16)
    test_basis = normal_values(splits[1], (DOMAINS, 2, TEST_DEV, NB), DOM_PTS ** -0.5, 0.25, ((0, 256),))
    source_points = jnp.clip(4.0 * jax.random.uniform(splits[2], (DOMAINS, 3, SRC_PTS), jnp.float32) ** level_of(splits[2], (DOMAINS, 3, SRC_PTS), ((0, 256),), -0.2, 0.2), 0.0, 4.0).astype(jnp.bfloat16)
    source_basis = normal_values(splits[3], (DOMAINS, 2, SRC_PTS, NB), SRC_PTS ** -0.5, 0.1875, ((0, 256),))
    excitation = normal_values(splits[4], (DOMAINS, 2, NB, EXC), 1.0, 6.0, ((0, 256),))
    preconditioner = normal_values(splits[5], (DOMAINS, NB, 2, NB), (2 * NB) ** -0.5, 0.25, ((0, 256),))
    plan = draw_plan(jax.random.fold_in(splits[8], 71), 0)
    solver_owner = draw_solver_owner(jax.random.fold_in(splits[8], 71), 0)
    return {"test_points": test_points, "test_basis": test_basis, "source_points": source_points, "source_basis": source_basis, "excitation": excitation, "preconditioner": preconditioner, "plan": plan, "solver_owner": solver_owner}


wave_number = 2.0 * math.pi
wire_radius = 0.05

def green_parts(points_test, points_source):
    near = points_test.astype(jnp.float32)
    far = points_source.astype(jnp.float32)
    dist_sq = jnp.zeros((near.shape[1], far.shape[1]), jnp.float32)
    for component in range(3):
        offset = near[component][:, None] - far[component][None, :]
        dist_sq = dist_sq + offset * offset
    distance = jnp.sqrt(dist_sq + wire_radius * wire_radius)
    weight = 1.0 / (4.0 * math.pi * distance)
    green_re = (jnp.cos(wave_number * distance) * weight).astype(jnp.bfloat16)
    green_im = (-jnp.sin(wave_number * distance) * weight).astype(jnp.bfloat16)
    return (green_re, green_im)

def product(left, right):
    return jnp.dot(left, right, preferred_element_type=jnp.float32)

def reference(test_points, test_basis, source_points, source_basis, excitation, preconditioner, plan, solver_owner):
    owners = plan.reshape(-1).astype(jnp.int32)
    n_sources = owners.shape[0]
    per_domain = TEST_DEV // DOM_DEV
    far_points = source_points[owners]
    far_basis = source_basis[owners]
    far_coeff = excitation[owners]

    def one_device(index, assembled):
        own_points = test_points[index]
        own_basis = test_basis[index]
        group_base = index // N_MEMBER * N_MEMBER
        for source_slot in range(n_sources):
            green_re, green_im = green_parts(own_points, far_points[source_slot])
            basis_re = far_basis[source_slot, 0]
            basis_im = far_basis[source_slot, 1]
            half_re = (product(green_re, basis_re) - product(green_im, basis_im)).astype(jnp.bfloat16)
            half_im = (product(green_re, basis_im) + product(green_im, basis_re)).astype(jnp.bfloat16)
            coeff_re = far_coeff[source_slot, 0]
            coeff_im = far_coeff[source_slot, 1]
            for domain in range(DOM_DEV):
                start = domain * per_domain
                test_re = own_basis[0, start:start + per_domain]
                test_im = own_basis[1, start:start + per_domain]
                part_re = half_re[start:start + per_domain]
                part_im = half_im[start:start + per_domain]
                tile_re = (product(test_re.T, part_re) + product(test_im.T, part_im)).astype(jnp.bfloat16)
                tile_im = (product(test_re.T, part_im) - product(test_im.T, part_re)).astype(jnp.bfloat16)
                out_re = product(tile_re, coeff_re) - product(tile_im, coeff_im)
                out_im = product(tile_re, coeff_im) + product(tile_im, coeff_re)
                target = (group_base + solver_owner[index, domain, source_slot]).astype(jnp.int32)
                assembled = assembled.at[target].add(jnp.concatenate([out_re, out_im], axis=1))
        return assembled
    start_sum = jnp.zeros((DOMAINS, NB, 2 * EXC), jnp.float32)
    assembled = lax.fori_loop(0, DOMAINS, one_device, start_sum)
    assembled_low = assembled.astype(jnp.bfloat16)
    z_re = assembled_low[:, :, :EXC].astype(jnp.float32)
    z_im = assembled_low[:, :, EXC:].astype(jnp.float32)
    inv_re = preconditioner[:, :, 0, :].astype(jnp.float32)
    inv_im = preconditioner[:, :, 1, :].astype(jnp.float32)
    res_re = jnp.einsum('obk,oke->obe', inv_re, z_re) - jnp.einsum('obk,oke->obe', inv_im, z_im)
    res_im = jnp.einsum('obk,oke->obe', inv_re, z_im) + jnp.einsum('obk,oke->obe', inv_im, z_re)
    return jnp.stack([res_re, res_im], axis=2)
```

```python
import functools
import math

import jax
import jax.numpy as jnp
from jax import lax
from jax.experimental import pallas as pl
from jax.experimental.pallas import tpu as pltpu
from jax.sharding import PartitionSpec as P

MESH = pl.DeviceIdType.MESH
BF = jnp.bfloat16
F32 = jnp.float32

SIN = (0.07765591, -0.59829041, 2.55007739, -5.16771008, 3.14159264)
COS = (0.21968242, -1.33187297, 4.05841079, -4.9347928, 0.99999995)
RADIUS_SQ = 0.05 * 0.05

PTS = 1024
NB = 256
NX, NY, NZ = 4, 4, 8
PLANE = NX * NY * 2


def poly(coefficients, u):
    total = coefficients[0] * u + coefficients[1]
    for value in coefficients[2:]:
        total = total * u + value
    return total


def split3(value):
    high = value.astype(BF).astype(F32)
    rest = value - high
    mid = rest.astype(BF).astype(F32)
    return high, mid, rest - mid


def augment(points, store, is_source):
    centred = points.astype(F32) - 2.0
    h, m, l = split3(centred)
    size = jnp.sum(centred * centred, axis=0, keepdims=True)
    if not is_source:
        size = size + RADIUS_SQ
    sh, sm, sl = split3(size)
    ones = jnp.ones_like(sh)
    if is_source:
        parts = (h, m, h, m, l, h)
        tail = (ones, ones, ones, sh, sm, sl)
    else:
        parts = tuple(-2.0 * v for v in (h, h, m, m, h, l))
        tail = (sh, sm, sl, ones, ones, ones)
    row = 0
    for part in parts:
        store[row:row + 3, :] = part
        row += 3
    for part in tail:
        store[row:row + 1, :] = part
        row += 1
    store[row:row + 8, :] = jnp.zeros((8, part.shape[1]), F32)


def body(
    plan, owner_smem, owner_vec, test_pts, kb, src_pts, jb, xb,
    zblk,
    bundle, recv1, sel, recv2, fin, full,
    pt_recv, pt_sel, pt_z, test_all, kall, owner_rem, owner_other,
    aug_stage, aug_test, aug_src, d2buf, gre, gim, prod,
    pair_snd, pair_rcv, ch_snd, ch_rcv, table,
    p1_s, p1_r, s1_s, s1_r, p2_s, p2_r, s2_s, s2_r, s3_s, s3_r,
    s4_s, s4_r, k_s, k_r, pair_s, pair_r, ch_s, ch_r, loc,
):
    g = lax.axis_index("group")
    m = lax.axis_index("member")
    x, y = lax.rem(g, NX), lax.div(g, NX)
    c, z = lax.rem(m, 2), lax.div(m, 2)
    q = g * 2 + c
    other = 1 - c
    partner = (g, z * 2 + other)

    def remote(src, dst, send, recv, device):
        return pltpu.make_async_remote_copy(
            src_ref=src, dst_ref=dst, send_sem=send, recv_sem=recv,
            device_id=device, device_id_type=MESH,
        )

    def plane_peer(i):
        target = lax.rem(q + i, PLANE)
        return lax.div(target, 2), lax.rem(target, 2)

    def member_peer(i):
        return lax.rem(m + i, 2 * NZ)

    barrier = pltpu.get_barrier_semaphore()

    @pl.loop(1, PLANE)
    def _(i):
        tg, tc = plane_peer(i)
        pl.semaphore_signal(barrier, inc=1, device_id=(tg, z * 2 + tc), device_id_type=MESH)

    @pl.loop(1, 2 * NZ)
    def _(i):
        pl.semaphore_signal(barrier, inc=1, device_id=(g, member_peer(i)), device_id_type=MESH)

    pl.semaphore_wait(barrier, PLANE - 1 + 2 * NZ - 1)

    @pl.loop(1, PLANE)
    def _(i):
        tg, tc = plane_peer(i)
        remote(src_pts, pt_recv.at[q], p1_s, p1_r, (tg, z * 2 + tc)).start()

    pt_recv[q] = src_pts[...]

    k_copies = [
        remote(test_pts, test_all.at[1], k_s.at[0], k_r.at[0], partner),
        remote(owner_vec, owner_rem, k_s.at[1], k_r.at[1], partner),
    ]
    for copy in k_copies:
        copy.start()
    test_all[0] = test_pts[...]

    @pl.loop(0, 4)
    def _(b):
        rows = pl.ds(pl.multiple_of(b * 256, 256), 256)
        jr, ji = jb[0, rows, :], jb[1, rows, :]
        xr, xi = xb[0], xb[1]
        dot = functools.partial(jnp.dot, preferred_element_type=F32)
        re = dot(jr, xr) - dot(ji, xi)
        im = dot(jr, xi) + dot(ji, xr)
        bundle[pl.ds(b * 4, 4), :, 0:NB] = re.astype(BF).reshape(4, 64, NB)
        bundle[pl.ds(b * 4, 4), :, NB:2 * NB] = im.astype(BF).reshape(4, 64, NB)

    def half_cols(which):
        return pl.ds(pl.multiple_of(which * NB, NB), NB)

    @pl.loop(1, PLANE)
    def _(i):
        tg, tc = plane_peer(i)
        remote(
            bundle.at[tg, :, half_cols(tc)], recv1.at[q], s1_s, s1_r, (tg, z * 2 + tc)
        ).start()

    keep = pltpu.make_async_copy(bundle.at[g, :, half_cols(c)], recv1.at[q], loc.at[0])
    keep.start()

    k_big = remote(kb, kall.at[1], k_s.at[2], k_r.at[2], partner)
    k_big.start()
    k_own = pltpu.make_async_copy(kb, kall.at[0], loc.at[1])
    k_own.start()

    def wait_bytes(ref, send, recv):
        done = remote(ref, ref, send, recv, partner)
        done.wait_recv()
        done.wait_send()

    wait_bytes(pt_recv.at[pl.ds(0, PLANE - 1)], p1_s, p1_r)

    def plane_of(owner):
        return lax.div(owner, 2 * NZ) * 2 + lax.rem(owner, 2)

    def z_of(owner):
        return lax.div(lax.rem(owner, 2 * NZ), 2)

    for s in range(2):
        pt_sel[s] = pt_recv[plane_of(plan[c, s])]

    @pl.loop(1, NZ)
    def _(i):
        tz = lax.rem(z + i, NZ)
        remote(pt_sel, pt_z.at[z], p2_s, p2_r, (g, tz * 2 + c)).start()

    for s in range(2):
        pt_z[z, s] = pt_sel[s]

    wait_bytes(recv1.at[pl.ds(0, PLANE - 1)], s1_s, s1_r)
    keep.wait()
    for j in range(4):
        qj = plane_of(plan[j // 2, j % 2])
        for zp in range(NZ):
            r0, c0 = (zp % 4) * 16, (zp // 4) * 128
            sel[zp * 4 + j] = recv1[qj, r0:r0 + 16, c0:c0 + 128]

    @pl.loop(1, NZ)
    def _(i):
        tz = lax.rem(z + i, NZ)
        remote(
            sel.at[pl.ds(tz * 4, 4)], recv2.at[pl.ds(z * 4, 4)], s2_s, s2_r, (g, tz * 2 + c)
        ).start()

    recv2[pl.ds(z * 4, 4)] = sel[pl.ds(z * 4, 4)]

    wait_bytes(pt_z.at[pl.ds(0, NZ - 1)], p2_s, p2_r)
    k_copies[0].wait_recv()
    for s in range(2):
        augment(pt_z[z_of(plan[c, s]), s], aug_stage, True)
        aug_src[s] = aug_stage[...].astype(BF)
        augment(test_all[s], aug_stage, False)
        aug_test[s] = aug_stage[...].astype(BF)

    def green(first, last):
        @pl.loop(first, last)
        def _(unit):
            s, rest = lax.div(unit, 8), lax.rem(unit, 8)
            who, blk = lax.div(rest, 4), lax.rem(rest, 4)
            rows = pl.ds(pl.multiple_of(blk * 256, 256), 256)
            d2buf[...] = lax.dot_general(
                aug_test[who, :, rows], aug_src[s],
                (((0,), (0,)), ((), ())), preferred_element_type=F32,
            )
            base = rest * 256

            @pl.loop(0, 16)
            def _(r):
                row = pl.ds(pl.multiple_of(r * 16, 16), 16)
                out = pl.ds(pl.multiple_of(base + r * 16, 16), 16)
                for col in range(0, PTS, 512):
                    d2 = jnp.maximum(d2buf[row, col:col + 512], RADIUS_SQ)
                    inv = lax.rsqrt(d2)
                    dist = d2 * inv
                    f = dist - jnp.round(dist)
                    u = f * f
                    sn = poly(SIN, u) * f
                    cs = poly(COS, u)
                    t = (inv * (0.5 / math.pi)) * sn
                    re = inv * (0.25 / math.pi) - t * sn
                    gre[s, out, col:col + 512] = re.astype(BF)
                    gim[s, out, col:col + 512] = (t * cs).astype(BF)

    green(0, 3)

    wait_bytes(recv2.at[pl.ds(0, 4 * (NZ - 1))], s2_s, s2_r)
    for j in range(4):
        fin[j] = recv2[z_of(plan[j // 2, j % 2]) * 4 + j]

    my_rows = pl.ds(pl.multiple_of(lax.rem(z, 4) * 16, 16), 16)
    my_cols = pl.ds(pl.multiple_of(c * NB + lax.div(z, 4) * 128, 128), 128)
    home = full.at[:, y, x, my_rows, my_cols]

    @pl.loop(1, 2 * NZ)
    def _(i):
        tm = member_peer(i)
        remote(fin.at[pl.ds(lax.rem(tm, 2) * 2, 2)], home, s3_s, s3_r, (g, tm)).start()

    keep3 = pltpu.make_async_copy(fin.at[pl.ds(c * 2, 2)], home, loc.at[2])
    keep3.start()
    green(3, 6)
    wait_bytes(recv2.at[pl.ds(0, 2 * (2 * NZ - 1))], s3_s, s3_r)
    keep3.wait()

    cols = (slice(0, NB), slice(NB, 2 * NB))

    def at_y(value):
        return (value * NX + x, m)

    def at_x(value):
        return (y * NX + value, m)

    xp, xm = lax.rem(x + 1, NX), lax.rem(x + NX - 1, NX)
    yp, ym = lax.rem(y + 1, NY), lax.rem(y + NY - 1, NY)
    started = []

    def send4(ref, index, device):
        copy = remote(ref, ref, s4_s.at[index], s4_r.at[index], device)
        copy.start()
        started.append(copy)
        return copy

    up, down = pl.ds(0, 32), pl.ds(32, 32)
    a = [
        send4(full.at[:, y, x, :, cols[0]], 0, at_y(yp)),
        send4(full.at[:, y, x, :, cols[0]], 1, at_y(ym)),
        send4(full.at[:, y, x, :, cols[1]], 2, at_x(xp)),
        send4(full.at[:, y, x, :, cols[1]], 3, at_x(xm)),
    ]
    green(6, 8)
    a[0].wait_recv()
    b = [send4(full.at[:, ym, x, up, cols[0]], 4, at_y(yp))]
    a[2].wait_recv()
    b.append(send4(full.at[:, y, xm, up, cols[1]], 5, at_x(xp)))
    a[1].wait_recv()
    b.append(send4(full.at[:, yp, x, down, cols[0]], 6, at_y(ym)))
    a[3].wait_recv()
    b.append(send4(full.at[:, y, xp, down, cols[1]], 7, at_x(xm)))
    green(8, 10)
    for copy in b:
        copy.wait_recv()
    d = []
    for s in range(2):
        k = 8 + 8 * s
        d.append([
            send4(full.at[s, :, x, :, cols[0]], k, at_x(xp)),
            send4(full.at[s, :, x, :, cols[0]], k + 1, at_x(xm)),
            send4(full.at[s, y, :, :, cols[1]], k + 2, at_y(yp)),
            send4(full.at[s, y, :, :, cols[1]], k + 3, at_y(ym)),
        ])
    lo, hi = pl.ds(0, 2), pl.ds(2, 2)
    e = []
    green(10, 13)
    for s in range(2):
        k = 12 + 8 * s
        d[s][0].wait_recv()
        e.append(send4(full.at[s, lo, xm, :, cols[0]], k, at_x(xp)))
        d[s][2].wait_recv()
        e.append(send4(full.at[s, ym, lo, :, cols[1]], k + 1, at_y(yp)))
        d[s][1].wait_recv()
        e.append(send4(full.at[s, hi, xp, :, cols[0]], k + 2, at_x(xm)))
        d[s][3].wait_recv()
        e.append(send4(full.at[s, yp, hi, :, cols[1]], k + 3, at_y(ym)))
        green(13 + 2 * s, 15 + s)
    k_big.wait_recv()
    k_own.wait()

    for s in range(2):
        for copy in e[4 * s:4 * s + 4]:
            copy.wait_recv()

        @pl.loop(0, 4)
        def _(dom, s=s):
            rows = pl.ds(pl.multiple_of(dom * 512, 512), 512)
            who = lax.div(dom, 2)
            krow = pl.ds(pl.multiple_of(lax.rem(dom, 2) * 512, 512), 512)
            basis = full[s].reshape(PTS, 2 * NB)
            dot = functools.partial(jnp.dot, preferred_element_type=F32)
            one = dot(gre[s, rows, :], basis)
            two = dot(gim[s, rows, :], basis)
            half_re = (one[:, :NB] + two[:, NB:]).astype(BF)
            half_im = (one[:, NB:] - two[:, :NB]).astype(BF)
            right = jnp.concatenate([half_re, half_im], axis=1)
            turned = jnp.concatenate([half_im, -half_re], axis=1)
            over = (((0,), (0,)), ((), ()))
            prod[s * 4 + dom] = lax.dot_general(
                kall[who, 0, krow, :], right, over, preferred_element_type=F32
            ) + lax.dot_general(
                kall[who, 1, krow, :], turned, over, preferred_element_type=F32
            )

    k_copies[1].wait_recv()
    scal = pltpu.make_async_copy(owner_rem, owner_other, loc.at[3])
    scal.start()

    @pl.loop(0, NB // 16)
    def _(i):
        prod[8, pl.ds(pl.multiple_of(i * 16, 16), 16), :] = jnp.zeros((16, 2 * NB), F32)

    scal.wait()
    owners = []
    for s in range(2):
        for dom in range(4):
            ref = owner_smem if dom < 2 else owner_other
            owners.append(ref[dom % 2, 2 * c + s])

    @pl.loop(0, 2 * NZ)
    def _(slot):
        chosen = [jnp.int32(8)] * 4
        for t in range(7, -1, -1):
            hit = owners[t] == slot
            chosen = [
                jnp.where(hit, new, old)
                for old, new in zip(chosen, [jnp.int32(t)] + chosen[:3])
            ]
        for k in range(4):
            table[slot * 4 + k] = chosen[k]

    def combine(write, zz, cc, start, count, extras):
        base = (zz * 2 + cc) * 4
        picks = [table[base + k] for k in range(4)]

        @pl.loop(0, count // 16)
        def _(i):
            near = pl.ds(pl.multiple_of(i * 16, 16), 16)
            rows = pl.ds(pl.multiple_of(start + i * 16, 16), 16)
            total = prod[picks[0], rows, :] + prod[picks[1], rows, :]
            total = total + (prod[picks[2], rows, :] + prod[picks[3], rows, :])
            for ref, shifted in extras:
                total = total + ref[near if shifted else rows, :].astype(F32)
            write(near, rows, total)

    def to_slot(dz):
        return lax.rem(z + dz + NZ, NZ)

    pair_copies = {}

    def pair_send(dz):
        zz = to_slot(dz)
        index = dz % NZ

        def write(near, rows, total):
            pair_snd[index, rows, :] = total.astype(BF)

        combine(write, zz, other, 0, NB, ())
        copy = remote(
            pair_snd.at[index], pair_rcv.at[index],
            pair_s.at[index], pair_r.at[index], partner,
        )
        copy.start()
        pair_copies[index] = copy

    waited = set()

    def pair_ready(dz):
        index = dz % NZ
        if index not in waited:
            waited.add(index)
            pair_copies[index].wait_recv()
        return pair_rcv.at[index]

    ahead = (g, lax.rem(z + 1, NZ) * 2 + c)
    behind = (g, lax.rem(z + NZ - 1, NZ) * 2 + c)
    chains = ((4, 0, ahead), (3, 128, ahead), (-4, 128, behind), (-3, 0, behind))
    ch_copies = {}

    def chain_step(ch, k):
        far, start, device = chains[ch]
        steps = abs(far)
        if k >= steps:
            return
        dz = far - k if far > 0 else far + k
        extras = [(pair_ready(dz), False)]
        if k:
            ch_copies[ch, k - 1].wait_recv()
            extras.append((ch_rcv.at[ch, k - 1], True))

        def write(near, rows, total):
            ch_snd[ch, k, near, :] = total.astype(BF)

        combine(write, to_slot(dz), c, start, 128, extras)
        copy = remote(
            ch_snd.at[ch, k], ch_rcv.at[ch, k],
            ch_s.at[4 * ch + k], ch_r.at[4 * ch + k], device,
        )
        copy.start()
        ch_copies[ch, k] = copy

    order = (0, 2, 1, 3)
    pair_send(4)
    pair_send(3)
    pair_send(-3)
    for ch in order:
        chain_step(ch, 0)
    pair_send(2)
    pair_send(-2)
    for ch in order:
        chain_step(ch, 1)
    pair_send(1)
    pair_send(-1)
    pair_send(0)
    for ch in order:
        chain_step(ch, 2)
    for ch in order:
        chain_step(ch, 3)

    own = pair_ready(0)
    for start, last, side in ((0, (0, 3), (3, 2)), (128, (2, 3), (1, 2))):
        ch_copies[side].wait_recv()
        ch_copies[last].wait_recv()

        def write(near, rows, total):
            low = total.astype(BF)
            zr, zi = low[:, :NB], low[:, NB:]
            zblk[rows, :NB] = zr
            zblk[rows, NB:] = zi
            lower = pl.ds(pl.multiple_of(rows.start + NB, 16), 16)
            zblk[lower, :NB] = -zi
            zblk[lower, NB:] = zr

        combine(
            write, z, c, start, 128,
            [(own, False), (ch_rcv.at[side[0], side[1]], True),
             (ch_rcv.at[last[0], last[1]], True)],
        )

    for copy in k_copies + [k_big] + started:
        copy.wait_send()
    for copy in list(pair_copies.values()) + list(ch_copies.values()):
        copy.wait_send()


def reduced(test_points, test_basis, source_points, source_basis, excitation, plan, owner):
    vmem = pl.BlockSpec(memory_space=pltpu.VMEM)
    smem = pl.BlockSpec(memory_space=pltpu.SMEM)
    dma = pltpu.SemaphoreType.DMA
    scratch = [
        pltpu.VMEM((16, 64, 2 * NB), BF),
        pltpu.VMEM((PLANE, 64, NB), BF),
        pltpu.VMEM((4 * NZ, 16, 128), BF),
        pltpu.VMEM((4 * NZ, 16, 128), BF),
        pltpu.VMEM((4, 16, 128), BF),
        pltpu.VMEM((2, NY, NX, 64, 2 * NB), BF),
        pltpu.VMEM((PLANE, 3, PTS), BF),
        pltpu.VMEM((2, 3, PTS), BF),
        pltpu.VMEM((NZ, 2, 3, PTS), BF),
        pltpu.VMEM((2, 3, PTS), BF),
        pltpu.VMEM((2, 2, PTS, NB), BF),
        pltpu.VMEM((2, 4), jnp.int32),
        pltpu.SMEM((2, 4), jnp.int32),
        pltpu.VMEM((32, PTS), F32),
        pltpu.VMEM((2, 32, PTS), BF),
        pltpu.VMEM((2, 32, PTS), BF),
        pltpu.VMEM((256, PTS), F32),
        pltpu.VMEM((2, 2 * PTS, PTS), BF),
        pltpu.VMEM((2, 2 * PTS, PTS), BF),
        pltpu.VMEM((9, NB, 2 * NB), F32),
        pltpu.VMEM((NZ, NB, 2 * NB), BF),
        pltpu.VMEM((NZ, NB, 2 * NB), BF),
        pltpu.VMEM((4, 4, 128, 2 * NB), BF),
        pltpu.VMEM((4, 4, 128, 2 * NB), BF),
        pltpu.SMEM((4 * 2 * NZ,), jnp.int32),
        dma, dma, dma, dma, dma, dma, dma, dma, dma, dma,
        dma((24,)), dma((24,)), dma((3,)), dma((3,)),
        dma((NZ,)), dma((NZ,)), dma((16,)), dma((16,)), dma((4,)),
    ]
    return pl.pallas_call(
        body,
        out_shape=jax.ShapeDtypeStruct((2 * NB, 2 * NB), BF),
        in_specs=[
            smem, smem, vmem, vmem, pl.BlockSpec(memory_space=pl.ANY), vmem, vmem, vmem,
        ],
        out_specs=vmem,
        scratch_shapes=scratch,
        compiler_params=pltpu.CompilerParams(
            collective_id=0, has_side_effects=True, vmem_limit_bytes=60 * 1024 * 1024
        ),
    )(plan, owner, owner, test_points, test_basis, source_points, source_basis, excitation)


def shards(
    test_points,
    test_basis,
    source_points,
    source_basis,
    excitation,
    preconditioner,
    plan,
    solver_owner,
):
    block = reduced(
        test_points[0], test_basis[0], source_points[0], source_basis[0], excitation[0],
        plan, solver_owner[0],
    )
    rows = preconditioner[0].reshape(NB, 2 * NB)
    outcome = jnp.dot(rows, block, preferred_element_type=F32)
    return outcome.reshape(1, NB, 2, NB)


def solution(mesh):
    return jax.shard_map(
        shards,
        mesh=mesh,
        in_specs=(
            P(("group", "member"), None, None),
            P(("group", "member"), None, None, None),
            P(("group", "member"), None, None),
            P(("group", "member"), None, None, None),
            P(("group", "member"), None, None, None),
            P(("group", "member"), None, None, None),
            P(),
            P(("group", "member"), None, None),
        ),
        out_specs=P(("group", "member"), None, None, None),
        check_vma=False,
    )
```

```python
import functools
import math

import jax
import jax.numpy as jnp
from jax import lax
from jax.experimental import pallas as pl
from jax.experimental.pallas import tpu as pltpu
from jax.sharding import PartitionSpec as P

MESH = pl.DeviceIdType.MESH
BF = jnp.bfloat16
F32 = jnp.float32

SIN = (0.07765591, -0.59829041, 2.55007739, -5.16771008, 3.14159264)
COS = (0.21968242, -1.33187297, 4.05841079, -4.9347928, 0.99999995)
RADIUS_SQ = 0.05 * 0.05

PTS = 1024
NB = 256
HALF = NB // 2
NX, NY, NZ = 4, 4, 8
PLANE = NX * NY * 2


def poly(coefficients, u):
    total = coefficients[0] * u + coefficients[1]
    for value in coefficients[2:]:
        total = total * u + value
    return total


def split3(value):
    high = value.astype(BF).astype(F32)
    rest = value - high
    mid = rest.astype(BF).astype(F32)
    return high, mid, rest - mid


def augment(points, store, is_source):
    centred = points.astype(F32) - 2.0
    h, m, l = split3(centred)
    size = jnp.sum(centred * centred, axis=0, keepdims=True)
    if not is_source:
        size = size + RADIUS_SQ
    sh, sm, sl = split3(size)
    ones = jnp.ones_like(sh)
    if is_source:
        parts = (h, m, h, m, l, h)
        tail = (ones, ones, ones, sh, sm, sl)
    else:
        parts = tuple(-2.0 * v for v in (h, h, m, m, h, l))
        tail = (sh, sm, sl, ones, ones, ones)
    row = 0
    for part in parts:
        store[row:row + 3, :] = part
        row += 3
    for part in tail:
        store[row:row + 1, :] = part
        row += 1
    store[row:row + 8, :] = jnp.zeros((8, part.shape[1]), F32)


def body(
    plan, owner_smem, owner_vec, test_pts, kb, src_pts, jb_hbm, xb_hbm,
    zblk,
    jb, xb, bundle, recv1, sel, recv2, fin, full,
    pt_recv, pt_sel, pt_z, test_all, kall, owner_rem, owner_other,
    aug_stage, aug_test, aug_src, d2buf, gre, gim, prod,
    pair_snd, pair_rcv, ch_snd, ch_rcv, table,
    p1_s, p1_r, s1_s, s1_r, p2_s, p2_r, s2_s, s2_r, s3_s, s3_r,
    s4_s, s4_r, k_s, k_r, pair_s, pair_r, ch_s, ch_r, loc,
):
    g = lax.axis_index("group")
    m = lax.axis_index("member")
    x, y = lax.rem(g, NX), lax.div(g, NX)
    c, z = lax.rem(m, 2), lax.div(m, 2)
    q = g * 2 + c
    other = 1 - c
    partner = (g, z * 2 + other)
    dot = functools.partial(jnp.dot, preferred_element_type=F32)

    def remote(src, dst, send, recv, device):
        return pltpu.make_async_remote_copy(
            src_ref=src, dst_ref=dst, send_sem=send, recv_sem=recv,
            device_id=device, device_id_type=MESH,
        )

    def plane_peer(i):
        target = lax.rem(q + i, PLANE)
        return lax.div(target, 2), lax.rem(target, 2)

    def member_peer(i):
        return lax.rem(m + i, 2 * NZ)

    loads = [
        pltpu.make_async_copy(jb_hbm, jb, loc.at[0]),
        pltpu.make_async_copy(xb_hbm, xb, loc.at[1]),
    ]
    for copy in loads:
        copy.start()

    barrier = pltpu.get_barrier_semaphore()

    @pl.loop(1, 2 * NZ)
    def _(i):
        pl.semaphore_signal(barrier, inc=1, device_id=(g, member_peer(i)), device_id_type=MESH)

    @pl.loop(1, PLANE)
    def _(i):
        tg, tc = plane_peer(i)
        pl.semaphore_signal(barrier, inc=1, device_id=(tg, z * 2 + tc), device_id_type=MESH)

    for copy in loads:
        copy.wait()
    k_own = pltpu.make_async_copy(kb, kall.at[0], loc.at[2])
    k_own.start()

    @pl.loop(0, 4)
    def _(b):
        rows = pl.ds(pl.multiple_of(b * 256, 256), 256)
        jr, ji = jb[0, rows, :], jb[1, rows, :]
        xr, xi = xb[0], xb[1]
        re = (dot(jr, xr) - dot(ji, xi)).astype(BF)
        im = (dot(jr, xi) + dot(ji, xr)).astype(BF)
        for h in range(2):
            cols = slice(h * HALF, (h + 1) * HALF)
            bundle[h, pl.ds(b * 4, 4), :, 0:HALF] = re[:, cols].reshape(4, 64, HALF)
            bundle[h, pl.ds(b * 4, 4), :, HALF:NB] = im[:, cols].reshape(4, 64, HALF)

    pt_recv[q] = src_pts[...]
    test_all[0] = test_pts[...]

    pl.semaphore_wait(barrier, PLANE - 1 + 2 * NZ - 1)

    @pl.loop(1, PLANE)
    def _(i):
        tg, tc = plane_peer(i)
        remote(src_pts, pt_recv.at[q], p1_s, p1_r, (tg, z * 2 + tc)).start()

    for tc in range(2):
        @pl.when(c != tc)
        def _(tc=tc):
            remote(bundle.at[tc, g], recv1.at[q], s1_s, s1_r, (g, z * 2 + tc)).start()

        @pl.loop(1, NX * NY)
        def _(i, tc=tc):
            tg = lax.rem(g + i, NX * NY)
            remote(bundle.at[tc, tg], recv1.at[q], s1_s, s1_r, (tg, z * 2 + tc)).start()

    keep = pltpu.make_async_copy(bundle.at[c, g], recv1.at[q], loc.at[0])
    keep.start()

    k_copies = [
        remote(test_pts, test_all.at[1], k_s.at[0], k_r.at[0], partner),
        remote(owner_vec, owner_rem, k_s.at[1], k_r.at[1], partner),
        remote(kb, kall.at[1], k_s.at[2], k_r.at[2], partner),
    ]
    for copy in k_copies:
        copy.start()

    def wait_bytes(ref, send, recv):
        done = remote(ref, ref, send, recv, partner)
        done.wait_recv()
        done.wait_send()

    wait_bytes(pt_recv.at[pl.ds(0, PLANE - 1)], p1_s, p1_r)

    def plane_of(owner):
        return lax.div(owner, 2 * NZ) * 2 + lax.rem(owner, 2)

    def z_of(owner):
        return lax.div(lax.rem(owner, 2 * NZ), 2)

    for s in range(2):
        pt_sel[s] = pt_recv[plane_of(plan[c, s])]

    @pl.loop(1, NZ)
    def _(i):
        tz = lax.rem(z + i, NZ)
        remote(pt_sel, pt_z.at[z], p2_s, p2_r, (g, tz * 2 + c)).start()

    for s in range(2):
        pt_z[z, s] = pt_sel[s]

    k_copies[0].wait_recv()
    for s in range(2):
        augment(test_all[s], aug_stage, False)
        aug_test[s] = aug_stage[...].astype(BF)

    def recv_bytes(ref, recv):
        remote(ref, ref, s1_s, recv, partner).wait_recv()

    recv_bytes(recv1.at[pl.ds(0, PLANE - 1)], s1_r)
    keep.wait()
    for j in range(4):
        qj = plane_of(plan[j // 2, j % 2])
        for zp in range(NZ):
            r0, c0 = (zp % 4) * 16, (zp // 4) * 128
            sel[zp * 4 + j] = recv1[qj, r0:r0 + 16, c0:c0 + 128]

    @pl.loop(1, NZ)
    def _(i):
        tz = lax.rem(z + i, NZ)
        remote(
            sel.at[pl.ds(tz * 4, 4)], recv2.at[pl.ds(z * 4, 4)], s2_s, s2_r, (g, tz * 2 + c)
        ).start()

    recv2[pl.ds(z * 4, 4)] = sel[pl.ds(z * 4, 4)]

    wait_bytes(pt_z.at[pl.ds(0, NZ - 1)], p2_s, p2_r)
    for s in range(2):
        augment(pt_z[z_of(plan[c, s]), s], aug_stage, True)
        aug_src[s] = aug_stage[...].astype(BF)

    def green(first, last):
        @pl.loop(first, last)
        def _(unit):
            s, rest = lax.div(unit, 8), lax.rem(unit, 8)
            who, blk = lax.div(rest, 4), lax.rem(rest, 4)
            rows = pl.ds(pl.multiple_of(blk * 256, 256), 256)
            d2buf[...] = lax.dot_general(
                aug_test[who, :, rows], aug_src[s],
                (((0,), (0,)), ((), ())), preferred_element_type=F32,
            )
            base = rest * 256

            @pl.loop(0, 16)
            def _(r):
                row = pl.ds(pl.multiple_of(r * 16, 16), 16)
                out = pl.ds(pl.multiple_of(base + r * 16, 16), 16)
                for col in range(0, PTS, 512):
                    d2 = jnp.maximum(d2buf[row, col:col + 512], RADIUS_SQ)
                    inv = lax.rsqrt(d2)
                    dist = d2 * inv
                    f = dist - jnp.round(dist)
                    u = f * f
                    sn = poly(SIN, u) * f
                    cs = poly(COS, u)
                    t = (inv * (0.5 / math.pi)) * sn
                    re = inv * (0.25 / math.pi) - t * sn
                    gre[s, out, col:col + 512] = re.astype(BF)
                    gim[s, out, col:col + 512] = (t * cs).astype(BF)

    green(0, 2)

    wait_bytes(recv2.at[pl.ds(0, 4 * (NZ - 1))], s2_s, s2_r)
    for j in range(4):
        fin[j] = recv2[z_of(plan[j // 2, j % 2]) * 4 + j]

    my_rows = pl.ds(pl.multiple_of(lax.rem(z, 4) * 16, 16), 16)
    my_cols = pl.ds(pl.multiple_of(lax.div(z, 4) * 128, 128), 128)
    home = full.at[:, c, y, x, my_rows, my_cols]

    @pl.loop(1, 2 * NZ)
    def _(i):
        tm = member_peer(i)
        remote(
            fin.at[pl.ds(lax.rem(tm, 2) * 2, 2)], home, s3_s, s3_r.at[c], (g, tm)
        ).start()

    pltpu.make_async_copy(fin.at[pl.ds(c * 2, 2)], home, s3_r.at[c]).start()

    started = []
    arriving = {}

    def gather(h, stage):
        for pipe in range(2):
            along_y = pipe == stage
            if stage == 0:
                part = full.at[pipe, h, y, x]
            elif pipe == 0:
                part = full.at[0, h, :, x]
            else:
                part = full.at[1, h, y]
            for step in (1, 3, 2):
                if along_y:
                    device = (lax.rem(y + step, NY) * NX + x, m)
                else:
                    device = (y * NX + lax.rem(x + step, NX), m)
                index = ((h * 2 + stage) * 2 + pipe) * 3 + step - 1
                copy = remote(part, part, s4_s.at[index], s4_r.at[index], device)
                copy.start()
                started.append(copy)
                arriving.setdefault((h, stage), []).append(copy)

    def gathered(h, stage):
        for copy in arriving[h, stage]:
            copy.wait_recv()

    green(2, 6)
    recv_bytes(recv2.at[pl.ds(0, 2 * NZ)], s3_r.at[0])
    gather(0, 0)
    green(6, 8)
    recv_bytes(recv2.at[pl.ds(0, 2 * NZ)], s3_r.at[1])
    gather(1, 0)
    gathered(0, 0)
    gather(0, 1)
    green(8, 11)
    gathered(1, 0)
    gather(1, 1)
    green(11, 16)

    k_copies[1].wait_recv()
    scal = pltpu.make_async_copy(owner_rem, owner_other, loc.at[3])
    scal.start()
    for h in range(2):
        @pl.loop(0, NB // 16)
        def _(i, h=h):
            prod[h, 8, pl.ds(pl.multiple_of(i * 16, 16), 16), :] = jnp.zeros((16, NB), F32)

    scal.wait()
    owners = []
    for s in range(2):
        for dom in range(4):
            ref = owner_smem if dom < 2 else owner_other
            owners.append(ref[dom % 2, 2 * c + s])

    @pl.loop(0, 2 * NZ)
    def _(slot):
        chosen = [jnp.int32(8)] * 4
        for t in range(7, -1, -1):
            hit = owners[t] == slot
            chosen = [
                jnp.where(hit, new, old)
                for old, new in zip(chosen, [jnp.int32(t)] + chosen[:3])
            ]
        for k in range(4):
            table[slot * 4 + k] = chosen[k]

    k_copies[2].wait_recv()
    k_own.wait()

    def multiply(h, first, last):
        @pl.loop(first, last)
        def _(unit):
            s, dom = lax.div(unit, 4), lax.rem(unit, 4)
            rows = pl.ds(pl.multiple_of(dom * 512, 512), 512)
            who = lax.div(dom, 2)
            krow = pl.ds(pl.multiple_of(lax.rem(dom, 2) * 512, 512), 512)
            basis = full[s, h].reshape(PTS, NB)
            one = dot(gre[s, rows, :], basis)
            two = dot(gim[s, rows, :], basis)
            half_re = (one[:, :HALF] + two[:, HALF:]).astype(BF)
            half_im = (one[:, HALF:] - two[:, :HALF]).astype(BF)
            right = jnp.concatenate([half_re, half_im], axis=1)
            turned = jnp.concatenate([half_im, -half_re], axis=1)
            over = (((0,), (0,)), ((), ()))
            prod[h, unit] = lax.dot_general(
                kall[who, 0, krow, :], right, over, preferred_element_type=F32
            ) + lax.dot_general(
                kall[who, 1, krow, :], turned, over, preferred_element_type=F32
            )

    def combine(h, write, zz, cc, start, count, extras):
        base = (zz * 2 + cc) * 4
        picks = [table[base + k] for k in range(4)]

        @pl.loop(0, count // 32)
        def _(i):
            near = pl.ds(pl.multiple_of(i * 32, 32), 32)
            rows = pl.ds(pl.multiple_of(start + i * 32, 32), 32)
            total = prod[h, picks[0], rows, :] + prod[h, picks[1], rows, :]
            total = total + (prod[h, picks[2], rows, :] + prod[h, picks[3], rows, :])
            for ref, shifted in extras:
                total = total + ref[near if shifted else rows, :].astype(F32)
            write(near, rows, total)

    def to_slot(dz):
        return lax.rem(z + dz + NZ, NZ)

    pair_copies = {}
    waited = set()

    def pair_send(h, *distances):
        for dz in distances:
            index = h * NZ + dz % NZ

            def write(near, rows, total):
                pair_snd[index, rows, :] = total.astype(BF)

            combine(h, write, to_slot(dz), other, 0, NB, ())
            copy = remote(
                pair_snd.at[index], pair_rcv.at[index],
                pair_s.at[index], pair_r.at[index], partner,
            )
            copy.start()
            pair_copies[index] = copy

    def pair_ready(h, dz):
        index = h * NZ + dz % NZ
        if index not in waited:
            waited.add(index)
            pair_copies[index].wait_recv()
        return pair_rcv.at[index]

    ahead = (g, lax.rem(z + 1, NZ) * 2 + c)
    behind = (g, lax.rem(z + NZ - 1, NZ) * 2 + c)
    chains = ((4, 0, ahead), (3, 128, ahead), (-4, 128, behind), (-3, 0, behind))
    ch_copies = {}

    def chain_steps(h, k):
        for ch in (0, 2, 1, 3):
            far, start, device = chains[ch]
            if k >= abs(far):
                continue
            dz = far - k if far > 0 else far + k
            extras = [(pair_ready(h, dz), False)]
            index = (h * 4 + ch) * 4 + k
            if k:
                ch_copies[h, ch, k - 1].wait_recv()
                extras.append((ch_rcv.at[index - 1], True))

            def write(near, rows, total):
                ch_snd[index, near, :] = total.astype(BF)

            combine(h, write, to_slot(dz), c, start, 128, extras)
            copy = remote(
                ch_snd.at[index], ch_rcv.at[index], ch_s.at[index], ch_r.at[index], device
            )
            copy.start()
            ch_copies[h, ch, k] = copy

    def finish(h):
        own = pair_ready(h, 0)
        for start, last, side in ((0, (0, 3), (3, 2)), (128, (2, 3), (1, 2))):
            ch_copies[(h,) + side].wait_recv()
            ch_copies[(h,) + last].wait_recv()

            def write(near, rows, total):
                low = total.astype(BF)
                zr, zi = low[:, :HALF], low[:, HALF:]
                lower = pl.ds(pl.multiple_of(rows.start + NB, 32), 32)
                left = slice(h * HALF, (h + 1) * HALF)
                right = slice(NB + h * HALF, NB + (h + 1) * HALF)
                zblk[rows, left] = zr
                zblk[rows, right] = zi
                zblk[lower, left] = -zi
                zblk[lower, right] = zr

            combine(
                h, write, z, c, start, 128,
                [(own, False)] + [
                    (ch_rcv.at[(h * 4 + ch) * 4 + k], True) for ch, k in (side, last)
                ],
            )

    gathered(0, 1)
    multiply(0, 0, 8)
    pair_send(0, 4, 3, -3)
    chain_steps(0, 0)
    pair_send(0, 2, -2)
    gathered(1, 1)
    multiply(1, 0, 2)
    chain_steps(0, 1)
    pair_send(0, 1, -1, 0)
    multiply(1, 2, 4)
    chain_steps(0, 2)
    multiply(1, 4, 6)
    chain_steps(0, 3)
    multiply(1, 6, 8)
    pair_send(1, 4, 3, -3)
    chain_steps(1, 0)
    finish(0)
    pair_send(1, 2, -2)
    chain_steps(1, 1)
    pair_send(1, 1, -1, 0)
    chain_steps(1, 2)
    chain_steps(1, 3)
    finish(1)

    sent1 = recv1.at[pl.ds(0, PLANE - 1)]
    remote(sent1, sent1, s1_s, s1_r, partner).wait_send()
    sent3 = recv2.at[pl.ds(0, 2 * (2 * NZ - 1))]
    remote(sent3, sent3, s3_s, s1_r, partner).wait_send()
    for copy in k_copies + started:
        copy.wait_send()
    for copy in list(pair_copies.values()) + list(ch_copies.values()):
        copy.wait_send()


def reduced(test_points, test_basis, source_points, source_basis, excitation, plan, owner):
    vmem = pl.BlockSpec(memory_space=pltpu.VMEM)
    smem = pl.BlockSpec(memory_space=pltpu.SMEM)
    hbm = pl.BlockSpec(memory_space=pl.ANY)
    dma = pltpu.SemaphoreType.DMA
    scratch = [
        pltpu.VMEM((2, PTS, NB), BF),
        pltpu.VMEM((2, NB, NB), BF),
        pltpu.VMEM((2, 16, 64, NB), BF),
        pltpu.VMEM((PLANE, 64, NB), BF),
        pltpu.VMEM((4 * NZ, 16, 128), BF),
        pltpu.VMEM((4 * NZ, 16, 128), BF),
        pltpu.VMEM((4, 16, 128), BF),
        pltpu.VMEM((2, 2, NY, NX, 64, NB), BF),
        pltpu.VMEM((PLANE, 3, PTS), BF),
        pltpu.VMEM((2, 3, PTS), BF),
        pltpu.VMEM((NZ, 2, 3, PTS), BF),
        pltpu.VMEM((2, 3, PTS), BF),
        pltpu.VMEM((2, 2, PTS, NB), BF),
        pltpu.VMEM((2, 4), jnp.int32),
        pltpu.SMEM((2, 4), jnp.int32),
        pltpu.VMEM((32, PTS), F32),
        pltpu.VMEM((2, 32, PTS), BF),
        pltpu.VMEM((2, 32, PTS), BF),
        pltpu.VMEM((256, PTS), F32),
        pltpu.VMEM((2, 2 * PTS, PTS), BF),
        pltpu.VMEM((2, 2 * PTS, PTS), BF),
        pltpu.VMEM((2, 9, NB, NB), F32),
        pltpu.VMEM((2 * NZ, NB, NB), BF),
        pltpu.VMEM((2 * NZ, NB, NB), BF),
        pltpu.VMEM((32, 128, NB), BF),
        pltpu.VMEM((32, 128, NB), BF),
        pltpu.SMEM((4 * 2 * NZ,), jnp.int32),
        dma, dma, dma, dma, dma, dma, dma, dma, dma, dma((2,)),
        dma((24,)), dma((24,)), dma((3,)), dma((3,)),
        dma((2 * NZ,)), dma((2 * NZ,)), dma((32,)), dma((32,)), dma((4,)),
    ]
    return pl.pallas_call(
        body,
        out_shape=jax.ShapeDtypeStruct((2 * NB, 2 * NB), BF),
        in_specs=[smem, smem, vmem, vmem, hbm, vmem, hbm, hbm],
        out_specs=vmem,
        scratch_shapes=scratch,
        compiler_params=pltpu.CompilerParams(
            collective_id=0, has_side_effects=True, vmem_limit_bytes=60 * 1024 * 1024
        ),
    )(plan, owner, owner, test_points, test_basis, source_points, source_basis, excitation)


def shards(
    test_points,
    test_basis,
    source_points,
    source_basis,
    excitation,
    preconditioner,
    plan,
    solver_owner,
):
    block = reduced(
        test_points[0], test_basis[0], source_points[0], source_basis[0], excitation[0],
        plan, solver_owner[0],
    )
    rows = preconditioner[0].reshape(NB, 2 * NB)
    outcome = jnp.dot(rows, block, preferred_element_type=F32)
    return outcome.reshape(1, NB, 2, NB)


def solution(mesh):
    return jax.shard_map(
        shards,
        mesh=mesh,
        in_specs=(
            P(("group", "member"), None, None),
            P(("group", "member"), None, None, None),
            P(("group", "member"), None, None),
            P(("group", "member"), None, None, None),
            P(("group", "member"), None, None, None),
            P(("group", "member"), None, None, None),
            P(),
            P(("group", "member"), None, None),
        ),
        out_specs=P(("group", "member"), None, None, None),
        check_vma=False,
    )
```

```python
import functools
import math

import jax
import jax.numpy as jnp
from jax import lax
from jax.experimental import pallas as pl
from jax.experimental.pallas import tpu as pltpu
from jax.sharding import PartitionSpec as P

MESH = pl.DeviceIdType.MESH
BF = jnp.bfloat16
F32 = jnp.float32

SIN = (0.07765591, -0.59829041, 2.55007739, -5.16771008, 3.14159264)
COS = (0.21968242, -1.33187297, 4.05841079, -4.9347928, 0.99999995)
RADIUS_SQ = 0.05 * 0.05

PTS = 1024
NB = 256
HALF = NB // 2
NX, NY, NZ = 4, 4, 8
PLANE = NX * NY * 2


def poly(coefficients, u):
    total = coefficients[0] * u + coefficients[1]
    for value in coefficients[2:]:
        total = total * u + value
    return total


def split3(value):
    high = value.astype(BF).astype(F32)
    rest = value - high
    mid = rest.astype(BF).astype(F32)
    return high, mid, rest - mid


def augment(points, store, is_source):
    centred = points.astype(F32) - 2.0
    h, m, l = split3(centred)
    size = jnp.sum(centred * centred, axis=0, keepdims=True)
    if not is_source:
        size = size + RADIUS_SQ
    sh, sm, sl = split3(size)
    ones = jnp.ones_like(sh)
    if is_source:
        parts = (h, m, h, m, l, h)
        tail = (ones, ones, ones, sh, sm, sl)
    else:
        parts = tuple(-2.0 * v for v in (h, h, m, m, h, l))
        tail = (sh, sm, sl, ones, ones, ones)
    row = 0
    for part in parts:
        store[row:row + 3, :] = part
        row += 3
    for part in tail:
        store[row:row + 1, :] = part
        row += 1
    store[row:row + 8, :] = jnp.zeros((8, part.shape[1]), F32)


def body(
    plan, owner_smem, owner_vec, test_pts, kb, src_pts, jb_hbm, xb_hbm,
    zblk,
    jb, xb, bundle, recv1, sel, recv2, fin, full,
    pt_recv, pt_sel, pt_z, test_all, kall, owner_rem, owner_other,
    aug_stage, aug_test, aug_src, d2buf, gre, gim, half, prod,
    pair_snd, pair_rcv, ch_snd, ch_rcv, table,
    p1_s, p1_r, s1_s, s1_r, p2_s, p2_r, s2_s, s2_r, s3_s, s3_r,
    s4_s, s4_r, k_s, k_r, pair_s, pair_r, ch_s, ch_r, loc,
):
    g = lax.axis_index("group")
    m = lax.axis_index("member")
    x, y = lax.rem(g, NX), lax.div(g, NX)
    c, z = lax.rem(m, 2), lax.div(m, 2)
    q = g * 2 + c
    other = 1 - c
    partner = (g, z * 2 + other)
    dot = functools.partial(jnp.dot, preferred_element_type=F32)

    def remote(src, dst, send, recv, device):
        return pltpu.make_async_remote_copy(
            src_ref=src, dst_ref=dst, send_sem=send, recv_sem=recv,
            device_id=device, device_id_type=MESH,
        )

    def plane_peer(i):
        target = lax.rem(q + i, PLANE)
        return lax.div(target, 2), lax.rem(target, 2)

    def member_peer(i):
        return lax.rem(m + i, 2 * NZ)

    loads = [
        pltpu.make_async_copy(jb_hbm, jb, loc.at[0]),
        pltpu.make_async_copy(xb_hbm, xb, loc.at[1]),
    ]
    for copy in loads:
        copy.start()

    barrier = pltpu.get_barrier_semaphore()

    @pl.loop(1, 2 * NZ)
    def _(i):
        pl.semaphore_signal(barrier, inc=1, device_id=(g, member_peer(i)), device_id_type=MESH)

    @pl.loop(1, PLANE)
    def _(i):
        tg, tc = plane_peer(i)
        pl.semaphore_signal(barrier, inc=1, device_id=(tg, z * 2 + tc), device_id_type=MESH)

    for copy in loads:
        copy.wait()
    k_own = pltpu.make_async_copy(kb, kall.at[0], loc.at[2])
    k_own.start()

    @pl.loop(0, 4)
    def _(b):
        rows = pl.ds(pl.multiple_of(b * 256, 256), 256)
        jr, ji = jb[0, rows, :], jb[1, rows, :]
        xr, xi = xb[0], xb[1]
        re = (dot(jr, xr) - dot(ji, xi)).astype(BF)
        im = (dot(jr, xi) + dot(ji, xr)).astype(BF)
        for h in range(2):
            cols = slice(h * HALF, (h + 1) * HALF)
            bundle[h, pl.ds(b * 4, 4), :, 0:HALF] = re[:, cols].reshape(4, 64, HALF)
            bundle[h, pl.ds(b * 4, 4), :, HALF:NB] = im[:, cols].reshape(4, 64, HALF)

    pt_recv[q] = src_pts[...]
    test_all[0] = test_pts[...]

    pl.semaphore_wait(barrier, PLANE - 1 + 2 * NZ - 1)

    @pl.loop(1, PLANE)
    def _(i):
        tg, tc = plane_peer(i)
        remote(src_pts, pt_recv.at[q], p1_s, p1_r, (tg, z * 2 + tc)).start()

    for tc in range(2):
        @pl.when(c != tc)
        def _(tc=tc):
            remote(bundle.at[tc, g], recv1.at[q], s1_s, s1_r, (g, z * 2 + tc)).start()

        @pl.loop(1, NX * NY)
        def _(i, tc=tc):
            tg = lax.rem(g + i, NX * NY)
            remote(bundle.at[tc, tg], recv1.at[q], s1_s, s1_r, (tg, z * 2 + tc)).start()

    keep = pltpu.make_async_copy(bundle.at[c, g], recv1.at[q], loc.at[0])
    keep.start()

    k_copies = [
        remote(test_pts, test_all.at[1], k_s.at[0], k_r.at[0], partner),
        remote(owner_vec, owner_rem, k_s.at[1], k_r.at[1], partner),
        remote(kb, kall.at[1], k_s.at[2], k_r.at[2], partner),
    ]
    for copy in k_copies:
        copy.start()

    def wait_bytes(ref, send, recv):
        done = remote(ref, ref, send, recv, partner)
        done.wait_recv()
        done.wait_send()

    wait_bytes(pt_recv.at[pl.ds(0, PLANE - 1)], p1_s, p1_r)

    def plane_of(owner):
        return lax.div(owner, 2 * NZ) * 2 + lax.rem(owner, 2)

    def z_of(owner):
        return lax.div(lax.rem(owner, 2 * NZ), 2)

    for s in range(2):
        pt_sel[s] = pt_recv[plane_of(plan[c, s])]

    @pl.loop(1, NZ)
    def _(i):
        tz = lax.rem(z + i, NZ)
        remote(pt_sel, pt_z.at[z], p2_s, p2_r, (g, tz * 2 + c)).start()

    for s in range(2):
        pt_z[z, s] = pt_sel[s]

    k_copies[0].wait_recv()
    for s in range(2):
        augment(test_all[s], aug_stage, False)
        aug_test[s] = aug_stage[...].astype(BF)

    def recv_bytes(ref, recv):
        remote(ref, ref, s1_s, recv, partner).wait_recv()

    def green(first, last):
        @pl.loop(first, last)
        def _(unit):
            s, rest = lax.div(unit, 8), lax.rem(unit, 8)
            who, blk = lax.div(rest, 4), lax.rem(rest, 4)
            rows = pl.ds(pl.multiple_of(blk * 256, 256), 256)
            d2buf[...] = lax.dot_general(
                aug_test[who, :, rows], aug_src[s],
                (((0,), (0,)), ((), ())), preferred_element_type=F32,
            )
            base = rest * 256

            @pl.loop(0, 8)
            def _(r):
                row = pl.ds(pl.multiple_of(r * 32, 32), 32)
                out = pl.ds(pl.multiple_of(base + r * 32, 32), 32)
                for col in range(0, PTS, 256):
                    d2 = jnp.maximum(d2buf[row, col:col + 256], RADIUS_SQ)
                    inv = lax.rsqrt(d2)
                    dist = d2 * inv
                    f = dist - jnp.round(dist)
                    u = f * f
                    sn = poly(SIN, u) * f
                    cs = poly(COS, u)
                    t = (inv * (0.5 / math.pi)) * sn
                    re = inv * (0.25 / math.pi) - t * sn
                    gre[s, out, col:col + 256] = re.astype(BF)
                    gim[s, out, col:col + 256] = (t * cs).astype(BF)

    recv_bytes(recv1.at[pl.ds(0, PLANE - 1)], s1_r)
    keep.wait()
    for j in range(4):
        qj = plane_of(plan[j // 2, j % 2])
        for zp in range(NZ):
            r0, c0 = (zp % 4) * 16, (zp // 4) * 128
            sel[zp * 4 + j] = recv1[qj, r0:r0 + 16, c0:c0 + 128]

    @pl.loop(1, NZ)
    def _(i):
        tz = lax.rem(z + i, NZ)
        remote(
            sel.at[pl.ds(tz * 4, 4)], recv2.at[pl.ds(z * 4, 4)], s2_s, s2_r, (g, tz * 2 + c)
        ).start()

    recv2[pl.ds(z * 4, 4)] = sel[pl.ds(z * 4, 4)]

    wait_bytes(pt_z.at[pl.ds(0, NZ - 1)], p2_s, p2_r)
    for s in range(2):
        augment(pt_z[z_of(plan[c, s]), s], aug_stage, True)
        aug_src[s] = aug_stage[...].astype(BF)


    wait_bytes(recv2.at[pl.ds(0, 4 * (NZ - 1))], s2_s, s2_r)
    for j in range(4):
        fin[j] = recv2[z_of(plan[j // 2, j % 2]) * 4 + j]

    my_rows = pl.ds(pl.multiple_of(lax.rem(z, 4) * 16, 16), 16)
    my_cols = pl.ds(pl.multiple_of(lax.div(z, 4) * 128, 128), 128)
    home = full.at[:, c, y, x, my_rows, my_cols]

    @pl.loop(1, 2 * NZ)
    def _(i):
        tm = member_peer(i)
        remote(
            fin.at[pl.ds(lax.rem(tm, 2) * 2, 2)], home, s3_s, s3_r.at[c], (g, tm)
        ).start()

    pltpu.make_async_copy(fin.at[pl.ds(c * 2, 2)], home, s3_r.at[c]).start()

    started = []
    arriving = {}

    def gather(h, stage):
        for pipe in range(2):
            along_y = pipe == stage
            if stage == 0:
                part = full.at[pipe, h, y, x]
            elif pipe == 0:
                part = full.at[0, h, :, x]
            else:
                part = full.at[1, h, y]
            for step in (1, 3, 2):
                if along_y:
                    device = (lax.rem(y + step, NY) * NX + x, m)
                else:
                    device = (y * NX + lax.rem(x + step, NX), m)
                index = ((h * 2 + stage) * 2 + pipe) * 3 + step - 1
                copy = remote(part, part, s4_s.at[index], s4_r.at[index], device)
                copy.start()
                started.append(copy)
                arriving.setdefault((h, stage), []).append(copy)

    def gathered(h, stage):
        for copy in arriving[h, stage]:
            copy.wait_recv()

    green(0, 16)
    recv_bytes(recv2.at[pl.ds(0, 2 * NZ)], s3_r.at[0])
    gather(0, 0)
    recv_bytes(recv2.at[pl.ds(0, 2 * NZ)], s3_r.at[1])
    gather(1, 0)
    gathered(0, 0)
    gather(0, 1)

    k_copies[1].wait_recv()
    scal = pltpu.make_async_copy(owner_rem, owner_other, loc.at[3])
    scal.start()
    for h in range(2):
        @pl.loop(0, NB // 16)
        def _(i, h=h):
            prod[h, 8, pl.ds(pl.multiple_of(i * 16, 16), 16), :] = jnp.zeros((16, NB), F32)

    scal.wait()
    owners = []
    for s in range(2):
        for dom in range(4):
            ref = owner_smem if dom < 2 else owner_other
            owners.append(ref[dom % 2, 2 * c + s])

    @pl.loop(0, 2 * NZ)
    def _(slot):
        chosen = [jnp.int32(8)] * 4
        for t in range(7, -1, -1):
            hit = owners[t] == slot
            chosen = [
                jnp.where(hit, new, old)
                for old, new in zip(chosen, [jnp.int32(t)] + chosen[:3])
            ]
        for k in range(4):
            table[slot * 4 + k] = chosen[k]

    k_copies[2].wait_recv()
    k_own.wait()
    gathered(1, 0)

    def field(h, unit):
        s, dom = lax.div(unit, 4), lax.rem(unit, 4)
        rows = pl.ds(pl.multiple_of(dom * 512, 512), 512)
        basis = full[s, h].reshape(PTS, NB)
        return dot(gre[s, rows, :], basis), dot(gim[s, rows, :], basis)

    def keep_field(slot, one, two):
        half[slot, :, :HALF] = (one[:, :HALF] + two[:, HALF:]).astype(BF)
        half[slot, :, HALF:] = (one[:, HALF:] - two[:, :HALF]).astype(BF)

    def project(h, unit, slot):
        dom = lax.rem(unit, 4)
        who = lax.div(dom, 2)
        krow = pl.ds(pl.multiple_of(lax.rem(dom, 2) * 512, 512), 512)
        right = half[slot]
        turned = jnp.concatenate([right[:, HALF:], -right[:, :HALF]], axis=1)
        over = (((0,), (0,)), ((), ()))
        prod[h, unit] = lax.dot_general(
            kall[who, 0, krow, :], right, over, preferred_element_type=F32
        ) + lax.dot_general(
            kall[who, 1, krow, :], turned, over, preferred_element_type=F32
        )

    def combine(h, write, zz, cc, start, count, extras):
        base = (zz * 2 + cc) * 4
        picks = [table[base + k] for k in range(4)]

        @pl.loop(0, count // 32)
        def _(i):
            near = pl.ds(pl.multiple_of(i * 32, 32), 32)
            rows = pl.ds(pl.multiple_of(start + i * 32, 32), 32)
            total = prod[h, picks[0], rows, :] + prod[h, picks[1], rows, :]
            total = total + (prod[h, picks[2], rows, :] + prod[h, picks[3], rows, :])
            for ref, shifted in extras:
                total = total + ref[near if shifted else rows, :].astype(F32)
            write(near, rows, total)

    def pair_copy(h, dz):
        index = h * NZ + dz
        return remote(
            pair_snd.at[index], pair_rcv.at[index],
            pair_s.at[index], pair_r.at[index], partner,
        )

    def pair_all(h):
        @pl.loop(0, NZ)
        def _(i):
            dz = 4 + lax.div(i + 1, 2) * (1 - 2 * lax.rem(i, 2))

            def write(near, rows, total):
                pair_snd[h * NZ + dz, rows, :] = total.astype(BF)

            combine(h, write, lax.rem(z + dz, NZ), other, 0, NB, ())
            pair_copy(h, dz).start()

    neighbours = (
        (g, lax.rem(z + 1, NZ) * 2 + c),
        (g, lax.rem(z + NZ - 1, NZ) * 2 + c),
    )

    def chain_base(h, side, pair):
        return ((h * 2 + side) * 2 + pair) * 5

    def chain_copy(index, side):
        return remote(
            ch_snd.at[index], ch_rcv.at[index + 1],
            ch_s.at[index], ch_r.at[index + 1], neighbours[side],
        )

    def chain_step(h, step):
        k, pair = lax.div(step, 2), lax.rem(step, 2)
        for side in range(2):
            far = 4 - pair - k
            dz = far if side == 0 else NZ - far
            start = 128 * pair if side == 0 else 128 * (1 - pair)
            index = chain_base(h, side, pair) + k
            fresh = step == 0 if side == 0 else step < 0

            @pl.when(jnp.logical_or(pair == 1, fresh))
            def _(dz=dz):
                pair_copy(h, dz).wait_recv()

            @pl.when(k > 0)
            def _(index=index, side=side):
                chain_copy(index - 1, side).wait_recv()

            def write(near, rows, total, index=index):
                ch_snd[index, near, :] = total.astype(BF)

            combine(
                h, write, lax.rem(z + dz, NZ), c, start, 128,
                [(pair_rcv.at[h * NZ + dz], False), (ch_rcv.at[index], True)],
            )
            chain_copy(index, side).start()

    def finish(h):
        pair_copy(h, 0).wait_recv()
        for part in range(2):
            last = chain_base(h, part, 0) + 4
            cross = chain_base(h, 1 - part, 1) + 3
            chain_copy(last - 1, part).wait_recv()
            chain_copy(cross - 1, 1 - part).wait_recv()

            def write(near, rows, total):
                low = total.astype(BF)
                zr, zi = low[:, :HALF], low[:, HALF:]
                lower = pl.ds(pl.multiple_of(rows.start + NB, 32), 32)
                left = pl.ds(pl.multiple_of(h * HALF, HALF), HALF)
                right = pl.ds(pl.multiple_of(NB + h * HALF, HALF), HALF)
                zblk[rows, left] = zr
                zblk[rows, right] = zi
                zblk[lower, left] = -zi
                zblk[lower, right] = zr

            combine(
                h, write, z, c, 128 * part, 128,
                [(pair_rcv.at[h * NZ], False), (ch_rcv.at[last], True), (ch_rcv.at[cross], True)],
            )

    @pl.loop(0, 8)
    def _(i):
        ch_rcv[i * 5] = jnp.zeros((128, NB), BF)

    gathered(0, 1)
    gather(1, 1)

    @pl.loop(0, 17)
    def _(step):
        @pl.when(step == 8)
        def _():
            gathered(1, 1)

        now = jnp.minimum(step, 15)
        old = jnp.maximum(step - 1, 0)
        one, two = field(lax.div(now, 8), lax.rem(now, 8))
        project(lax.div(old, 8), lax.rem(old, 8), lax.rem(step + 1, 2))
        keep_field(lax.rem(step, 2), one, two)

        @pl.when(step == 8)
        def _():
            pair_all(0)

        @pl.when(jnp.logical_and(step > 8, step < 16))
        def _():
            chain_step(0, step - 9)

    pair_all(1)

    @pl.loop(0, 7)
    def _(step):
        chain_step(1, step)

    @pl.loop(0, 2)
    def _(h):
        finish(h)

    @pl.loop(0, 2 * NZ)
    def _(i):
        pair_copy(0, i).wait_send()

    @pl.loop(0, 14)
    def _(i):
        h, step = lax.div(i, 7), lax.rem(i, 7)
        for side in range(2):
            index = chain_base(h, side, lax.rem(step, 2)) + lax.div(step, 2)
            chain_copy(index, side).wait_send()

    sent1 = recv1.at[pl.ds(0, PLANE - 1)]
    remote(sent1, sent1, s1_s, s1_r, partner).wait_send()
    sent3 = recv2.at[pl.ds(0, 2 * (2 * NZ - 1))]
    remote(sent3, sent3, s3_s, s1_r, partner).wait_send()
    for copy in k_copies + started:
        copy.wait_send()


def reduced(test_points, test_basis, source_points, source_basis, excitation, plan, owner):
    vmem = pl.BlockSpec(memory_space=pltpu.VMEM)
    smem = pl.BlockSpec(memory_space=pltpu.SMEM)
    hbm = pl.BlockSpec(memory_space=pl.ANY)
    dma = pltpu.SemaphoreType.DMA
    scratch = [
        pltpu.VMEM((2, PTS, NB), BF),
        pltpu.VMEM((2, NB, NB), BF),
        pltpu.VMEM((2, 16, 64, NB), BF),
        pltpu.VMEM((PLANE, 64, NB), BF),
        pltpu.VMEM((4 * NZ, 16, 128), BF),
        pltpu.VMEM((4 * NZ, 16, 128), BF),
        pltpu.VMEM((4, 16, 128), BF),
        pltpu.VMEM((2, 2, NY, NX, 64, NB), BF),
        pltpu.VMEM((PLANE, 3, PTS), BF),
        pltpu.VMEM((2, 3, PTS), BF),
        pltpu.VMEM((NZ, 2, 3, PTS), BF),
        pltpu.VMEM((2, 3, PTS), BF),
        pltpu.VMEM((2, 2, PTS, NB), BF),
        pltpu.VMEM((2, 4), jnp.int32),
        pltpu.SMEM((2, 4), jnp.int32),
        pltpu.VMEM((32, PTS), F32),
        pltpu.VMEM((2, 32, PTS), BF),
        pltpu.VMEM((2, 32, PTS), BF),
        pltpu.VMEM((256, PTS), F32),
        pltpu.VMEM((2, 2 * PTS, PTS), BF),
        pltpu.VMEM((2, 2 * PTS, PTS), BF),
        pltpu.VMEM((2, 512, NB), BF),
        pltpu.VMEM((2, 9, NB, NB), F32),
        pltpu.VMEM((2 * NZ, NB, NB), BF),
        pltpu.VMEM((2 * NZ, NB, NB), BF),
        pltpu.VMEM((40, 128, NB), BF),
        pltpu.VMEM((40, 128, NB), BF),
        pltpu.SMEM((4 * 2 * NZ,), jnp.int32),
        dma, dma, dma, dma, dma, dma, dma, dma, dma, dma((2,)),
        dma((24,)), dma((24,)), dma((3,)), dma((3,)),
        dma((2 * NZ,)), dma((2 * NZ,)), dma((40,)), dma((40,)), dma((4,)),
    ]
    return pl.pallas_call(
        body,
        out_shape=jax.ShapeDtypeStruct((2 * NB, 2 * NB), BF),
        in_specs=[smem, smem, vmem, vmem, hbm, vmem, hbm, hbm],
        out_specs=vmem,
        scratch_shapes=scratch,
        compiler_params=pltpu.CompilerParams(
            collective_id=0, has_side_effects=True, vmem_limit_bytes=60 * 1024 * 1024
        ),
    )(plan, owner, owner, test_points, test_basis, source_points, source_basis, excitation)


def shards(
    test_points,
    test_basis,
    source_points,
    source_basis,
    excitation,
    preconditioner,
    plan,
    solver_owner,
):
    block = reduced(
        test_points[0], test_basis[0], source_points[0], source_basis[0], excitation[0],
        plan, solver_owner[0],
    )
    rows = preconditioner[0].reshape(NB, 2 * NB)
    outcome = jnp.dot(rows, block, preferred_element_type=F32)
    return outcome.reshape(1, NB, 2, NB)


def solution(mesh):
    return jax.shard_map(
        shards,
        mesh=mesh,
        in_specs=(
            P(("group", "member"), None, None),
            P(("group", "member"), None, None, None),
            P(("group", "member"), None, None),
            P(("group", "member"), None, None, None),
            P(("group", "member"), None, None, None),
            P(("group", "member"), None, None, None),
            P(),
            P(("group", "member"), None, None),
        ),
        out_specs=P(("group", "member"), None, None, None),
        check_vma=False,
    )
```
